512 devices in a mesh: tm: 32 (over z_lo, x), wall: 16 (over z_hi, y, core).
Axes of the slice: x: 4, y: 4, z: 16 (z_hi: 2, z_lo: 8; z = z_hi * 8 + z_lo), core: 2. Of those that a mesh axis runs over, the one named last changes fastest.
Arguments:
- start_state: float32 [32, 3, 384, 2048], P('tm', None, 'wall'), may hold values from -6 to 6
- end_state: float32 [32, 3, 384, 2048], P('tm', None, None, 'wall'), may hold values from -6 to 6
- coupling: float32 [32, 3, 384, 2048], P('tm', None, None, 'wall'), may hold values from 0.5 to 1.5
- inverse_ops: float32 [32, 384, 384], P('wall')
- mirror_rows: int32 [384], replicated, may hold values from 0 to 383, as said below
- slab_steps: int32 [32], P('tm'), may hold values from 1 to 8, as said below
Outputs:
- gradient: float32 [32, 3, 384, 2048], P('tm', None, 'wall')
The draws below stay inside these ranges and needn't reach their ends.
Inputs may be any that keep to these rules, and one draw needn't show every extreme that they name: mirror_rows is an involution that maps each row of block b = y // 24 to a row of block 15 - b. `slab_steps`: some slab takes 8 steps.
All inputs are finite; a program needn't handle non-finite values.
Results may differ from the reference program's by a relative error of at most 0.00028.
Values sent between devices are 32-bit elements; how exact they have to be, the bound alone decides.
A program may use at most 64 MiB of HBM per device.

```python
import math
import jax
import jax.numpy as jnp
from jax import lax

NY = 384
STEPS_MAX = 8
ROWS_DEV = 24
GROUPS = 32
MODES = 2048
SLABS = 32


def draw_inverse_ops(key, part):
    first, second = jax.random.split(key)
    diagonal = jax.random.uniform(first, (GROUPS, NY), jnp.float32, 0.6, 1.0)
    spread = jax.random.normal(second, (GROUPS, NY, NY), jnp.float32)
    offdiag = spread * (0.35 / math.sqrt(NY))
    return offdiag + diagonal[:, :, None] * jnp.eye(NY, dtype=jnp.float32)[None, :, :]


def draw_mirror_rows(key, part):
    blocks_all = NY // ROWS_DEV
    half = blocks_all // 2
    keys = jax.random.split(key, half)
    perms = jax.vmap(lambda single: jax.random.permutation(single, ROWS_DEV))(keys).astype(jnp.int32)
    inverse = jnp.argsort(perms, axis=1).astype(jnp.int32)
    lower_blocks = jnp.arange(half, dtype=jnp.int32)[:, None]
    lower = (blocks_all - 1 - lower_blocks) * ROWS_DEV + perms
    upper = lower_blocks * ROWS_DEV + inverse
    return jnp.concatenate([lower.reshape(-1), upper[::-1].reshape(-1)]).astype(jnp.int32)


def draw_slab_steps(key, part):
    first, second = jax.random.split(key)
    short_most = max(STEPS_MAX // 4, 1)
    counts = jax.random.randint(first, (SLABS,), 1, short_most + 1)
    chosen = jax.random.randint(second, (), 0, SLABS)
    return jnp.where(jnp.arange(SLABS) == chosen, STEPS_MAX, counts).astype(jnp.int32)


def block_scale(key, shape, cuts, least, largest):
    gain, own = 1.0, jax.random.fold_in(key, 6)
    for axis_at, shards_of in cuts:
        draws = jnp.exp(jax.random.uniform(jax.random.fold_in(own, axis_at), (shards_of,), jnp.float32, least / len(cuts), largest / len(cuts)))
        gain = gain * jnp.repeat(draws, shape[axis_at] // shards_of).reshape([-1 if axis == axis_at else 1 for axis in range(len(shape))])
    return gain


def scatter_about(key, extent, width, bound, cuts=(), held_as=jnp.bfloat16):
    loudness = block_scale(key, extent, cuts, -0.22, 0.18) if cuts else 1.0
    result = jax.random.normal(key, extent, jnp.float32) * width * loudness
    return jnp.minimum(jnp.maximum(result, -bound), bound).astype(held_as)


def setup_inputs(seed: int = 0) -> dict:
    streams_of = jax.random.split(jax.random.key(seed), 7)
    start_state = scatter_about(streams_of[0], (SLABS, 3, NY, MODES), 1.0, 6.0, ((0, 32), (2, 16)), jnp.float32)
    end_state = scatter_about(streams_of[1], (SLABS, 3, NY, MODES), 1.0, 6.0, ((0, 32), (3, 16)), jnp.float32)
    coupling = jnp.clip(jnp.exp(math.log(1.5) - 1.0986123 * jax.random.uniform(streams_of[2], (SLABS, 3, NY, MODES), jnp.float32) ** block_scale(streams_of[2], (SLABS, 3, NY, MODES), ((0, 32), (3, 16)), -0.2, 0.2)), 0.5, 1.5)
    inverse_ops = draw_inverse_ops(jax.random.fold_in(streams_of[6], 71), 0)
    mirror_rows = draw_mirror_rows(jax.random.fold_in(streams_of[6], 71), 0)
    slab_steps = draw_slab_steps(jax.random.fold_in(streams_of[6], 71), 0)
    return {"start_state": start_state, "end_state": end_state, "coupling": coupling, "inverse_ops": inverse_ops, "mirror_rows": mirror_rows, "slab_steps": slab_steps}


def mirror(values, mirror_rows):
    parity = jnp.array([1.0, -1.0, 1.0], jnp.float32).reshape(1, 3, 1, 1)
    return jnp.take(values, mirror_rows, axis=2) * parity


def helmholtz(values, inverse_ops):
    slab_count, components, row_count, col_count = values.shape
    groups = inverse_ops.shape[0]
    blocked = values.reshape(slab_count, components, row_count, groups, col_count // groups)
    product = jnp.einsum("gyz,sczgm->scygm", inverse_ops, blocked, precision=lax.Precision.HIGHEST)
    return product.reshape(values.shape)


def reference(start_state, end_state, coupling, inverse_ops, mirror_rows, slab_steps):
    following = jnp.roll(start_state, -1, axis=0)
    mismatch = end_state - mirror(following, mirror_rows)
    adjoint_state = mismatch
    for position in range(STEPS_MAX):
        advanced = helmholtz(coupling * adjoint_state, inverse_ops)
        active = (position < slab_steps).reshape(-1, 1, 1, 1)
        adjoint_state = jnp.where(active, advanced, adjoint_state)
    earlier = mirror(jnp.roll(mismatch, 1, axis=0), mirror_rows)
    return adjoint_state - earlier
```

```python
import functools

import jax
import jax.numpy as jnp
from jax import lax
from jax.experimental import pallas as pl
from jax.experimental.pallas import tpu as pltpu
from jax.sharding import PartitionSpec as P

STEPS = 8
NY = 384
ROWS = 24
LANES = 128
WALL = 16
CHUNKS = ((0, 2), (2, 1))
SIGN = (1.0, -1.0, 1.0)
DETOUR = ((0, 0), (0, 1), (1, 0))
MESH = pl.DeviceIdType.MESH
F32 = jnp.float32
BF16 = jnp.bfloat16


def place():
    tm = lax.axis_index("tm")
    wall = lax.axis_index("wall")
    x = lax.rem(tm, 4)
    y = lax.rem(lax.div(wall, 2), 4)
    core = lax.rem(wall, 2)
    z = lax.div(wall, 8) * 8 + lax.div(tm, 4)
    return x, y, z, core


def device_at(x, y, z, core):
    x, y, z, core = lax.rem(x, 4), lax.rem(y, 4), lax.rem(z, 16), lax.rem(core, 2)
    return lax.rem(z, 8) * 4 + x, lax.div(z, 8) * 8 + y * 2 + core


def halves(value):
    high = value.astype(BF16)
    return high, (value - high.astype(F32)).astype(BF16)


def permuted(onehot, value):
    high = value.astype(BF16)
    rest = value - high.astype(F32)
    middle, low = halves(rest)
    dot = functools.partial(jnp.dot, preferred_element_type=F32)
    return (dot(onehot, high) + dot(onehot, middle)) + dot(onehot, low)


def kernel(start_ref, end_ref, coupling_ref, ops_ref, mirror_ref, steps_ref, out_ref,
           land, end_land, end_send, end_v, coup_v, ops_v, wcat, xcat, onehot, state, result,
           local_sem, send_sem, land_sem, end_sem, out_sem, own_sem):
    x, y, z, core = place()
    wall = lax.axis_index("wall")
    first = x == 0
    last = x == 3
    behind = jnp.where(first, 1, 0)
    z_next = lax.div(z, 8) * 8 + lax.rem(z + 1, 8)
    z_prev = lax.div(z, 8) * 8 + lax.rem(z + 7, 8)

    loads = [
        pltpu.make_async_copy(end_ref, end_v, local_sem.at[0]),
        pltpu.make_async_copy(ops_ref, ops_v, local_sem.at[1]),
        pltpu.make_async_copy(coupling_ref, coup_v, local_sem.at[2]),
    ]
    for load in loads:
        load.start()

    barrier = pltpu.get_barrier_semaphore()

    def greet(device):
        pl.semaphore_signal(barrier, inc=1, device_id=device, device_id_type=MESH)

    pairs = [(dy, dc) for dy in range(4) for dc in range(2)]
    ahead = jnp.where(last, 1, 0)
    for half in (8, 0):
        for dy, dc in pairs:
            greet(device_at(x + 3, y + dy, z + half + 16 - behind, core + dc))
            greet(device_at(x + 1, y + dy, z + half + ahead, core + dc))
            if half or dy or dc:
                greet(device_at(x, y + dy, z + half, core + dc))

    @pl.when(first)
    def _():
        for dy, dc in DETOUR:
            greet(device_at(x, y + dy, z + 14, core + dc))
            greet(device_at(x, y + 4 - dy, z + 2, core + dc))
        greet(device_at(x + 3, y, z + 9, core))
        greet(device_at(x + 1, y, z_prev, core))
        greet(device_at(x + 2, y, z_prev, core))

    @pl.when(last)
    def _():
        greet(device_at(x + 1, y, z + 7, core))
        greet(device_at(x + 2, y, z, core))
        greet(device_at(x + 3, y, z, core))

    @pl.when(x == 1)
    def _():
        greet(device_at(x + 2, y, z, core))
        greet(device_at(x + 3, y, z_next, core))

    @pl.when(x == 2)
    def _():
        greet(device_at(x + 1, y, z, core))
        greet(device_at(x + 2, y, z_next, core))

    extra = jnp.where(first, 2 * len(DETOUR) + 3, jnp.where(last, 3, 2))
    pl.semaphore_wait(barrier, 47 + extra)

    sends = []
    for index, (comp, count) in enumerate(CHUNKS):
        for half in (8, 0):
            order = pairs if not half else list(DETOUR) + [p for p in pairs if p not in DETOUR]
            for dy, dc in order:
                tm_to, wall_to = device_at(x + 3, y + dy, z + half + 16 - behind, core + dc)
                column = pl.multiple_of(wall_to * LANES, LANES)
                row, sem = wall * ROWS, index * (WALL + 3) + wall
                if half and (dy, dc) in DETOUR:
                    number = DETOUR.index((dy, dc))
                    tm_by, wall_by = device_at(x, y + dy, z + 14, core + dc)
                    tm_to = jnp.where(first, tm_by, tm_to)
                    wall_to = jnp.where(first, wall_by, wall_to)
                    row = jnp.where(first, NY + number * ROWS, row)
                    sem = jnp.where(first, index * (WALL + 3) + WALL + number, sem)
                send = pltpu.make_async_remote_copy(
                    start_ref.at[pl.ds(comp, count), :, pl.ds(column, LANES)],
                    land.at[pl.ds(comp, count), pl.ds(pl.multiple_of(row, 8), ROWS), :],
                    send_sem.at[0], land_sem.at[sem], device_id=(tm_to, wall_to), device_id_type=MESH)
                send.start()
                sends.append(send)

    lane = lax.broadcasted_iota(jnp.int32, (NY, LANES), 1)
    lower = lane < 64
    source = lax.broadcasted_iota(jnp.int32, (NY, NY), 0)
    onehot[...] = jnp.where(source == mirror_ref[...], 1.0, 0.0).astype(BF16)
    loads[0].wait()
    for comp in range(3):
        end_send[comp] = permuted(onehot[...], end_v[comp]) * SIGN[comp]
    for comp in range(3):
        slot, sem = comp, comp
        tm_to, wall_to = device_at(x + 1, y, jnp.where(last, z_next, z), core)
        if comp:
            tm_by, wall_by = device_at(x + 1 + comp, y, z, core)
            tm_to = jnp.where(last, tm_by, tm_to)
            wall_to = jnp.where(last, wall_by, wall_to)
            slot = jnp.where(last, 3, comp)
        send = pltpu.make_async_remote_copy(
            end_send.at[comp], end_land.at[slot], send_sem.at[1], end_sem.at[slot],
            device_id=(tm_to, wall_to), device_id_type=MESH)
        send.start()
        sends.append(send)
    loads[1].wait()
    for group in range(2):
        high, low = halves(ops_v[group])
        rows = slice(group * NY, (group + 1) * NY)
        wcat[rows, 0:NY] = high
        wcat[rows, NY:2 * NY] = low
        wcat[rows, 2 * NY:3 * NY] = high
    loads[2].wait()

    def arrival(ref, sem):
        return pltpu.make_async_remote_copy(
            ref, ref, send_sem.at[2], sem, device_id=(lax.axis_index("tm"), wall), device_id_type=MESH)

    def passing(index):
        comp, count = CHUNKS[index]
        copies = []
        for number, (dy, dc) in enumerate(DETOUR):
            _, wall_from = device_at(x, y + 4 - dy, z + 2, core + dc)
            held = land.at[pl.ds(comp, count), pl.ds(NY + number * ROWS, ROWS), :]
            copies.append((held, index * (WALL + 3) + WALL + number, pltpu.make_async_remote_copy(
                held, land.at[pl.ds(comp, count), pl.ds(pl.multiple_of(wall_from * ROWS, 8), ROWS), :],
                send_sem.at[2], land_sem.at[index * (WALL + 3) + wall_from],
                device_id=device_at(x + 3, y, z + 9, core), device_id_type=MESH)))
        return copies

    @pl.when(first)
    def _():
        for index in range(len(CHUNKS)):
            for held, sem, copy in passing(index):
                arrival(held, land_sem.at[sem]).wait_recv()
                copy.start()

    @pl.when((x == 1) | (x == 2))
    def _():
        arrival(end_land.at[3], end_sem.at[3]).wait_recv()
        pltpu.make_async_remote_copy(
            end_land.at[3], end_land.at[x], send_sem.at[2], end_sem.at[x],
            device_id=device_at(4 + x * 0, y, z_next, core), device_id_type=MESH).start()

    def leaving(index, half, dy, dc):
        comp, count = CHUNKS[index]
        tm_to, wall_to = device_at(x, y + dy, z + half, core + dc)
        return pltpu.make_async_remote_copy(
            result.at[pl.ds(comp, count), pl.ds(pl.multiple_of(wall_to * ROWS, 8), ROWS), :],
            out_ref.at[pl.ds(comp, count), :, pl.ds(pl.multiple_of(wall * LANES, LANES), LANES)],
            send_sem.at[3], out_sem.at[index * WALL + wall], device_id=(tm_to, wall_to), device_id_type=MESH)

    def staying(index):
        comp, count = CHUNKS[index]
        return pltpu.make_async_copy(
            result.at[pl.ds(comp, count), pl.ds(pl.multiple_of(wall * ROWS, 8), ROWS), :],
            out_ref.at[pl.ds(comp, count), :, pl.ds(pl.multiple_of(wall * LANES, LANES), LANES)],
            own_sem.at[index])

    steps = steps_ref[0]
    for index, (comp, count) in enumerate(CHUNKS):
        for place_from in range(WALL):
            arrival(land.at[pl.ds(comp, count), pl.ds(place_from * ROWS, ROWS), :],
                    land_sem.at[index * (WALL + 3) + place_from]).wait_recv()
        comps = range(comp, comp + count)
        width = count * LANES
        for at, c in enumerate(comps):
            state[:, at * LANES:(at + 1) * LANES] = end_v[c] - permuted(onehot[...], land[c, 0:NY, :]) * SIGN[c]

        def step(number, carry, comps=comps, width=width):
            for at, c in enumerate(comps):
                lanes = slice(at * LANES, (at + 1) * LANES)
                high, low = halves(coup_v[c] * state[:, lanes])
                xcat[0:NY, lanes] = high
                xcat[NY:2 * NY, lanes] = high
                xcat[2 * NY:3 * NY, lanes] = low
            both = jnp.dot(wcat[...], xcat[:, 0:width], preferred_element_type=F32)
            for at, c in enumerate(comps):
                lanes = slice(at * LANES, (at + 1) * LANES)
                advanced = jnp.where(lower, both[0:NY, lanes], both[NY:2 * NY, lanes])
                state[:, lanes] = jnp.where(number < steps, advanced, state[:, lanes])
            return carry

        lax.fori_loop(0, STEPS, step, 0)
        for at, c in enumerate(comps):
            arrival(end_land.at[c], end_sem.at[c]).wait_recv()
            result[c] = state[:, at * LANES:(at + 1) * LANES] - end_land[c]
        for half in (8, 0):
            for dy, dc in pairs:
                if half or dy or dc:
                    leaving(index, half, dy, dc).start()
        staying(index).start()

    for index, (comp, count) in enumerate(CHUNKS):
        staying(index).wait()
        for half in (8, 0):
            for dy, dc in pairs:
                if half or dy or dc:
                    _, wall_from = device_at(x, y + dy, z + half, core + dc)
                    arrival(out_ref.at[pl.ds(comp, count), :, pl.ds(pl.multiple_of(wall_from * LANES, LANES), LANES)],
                            out_sem.at[index * WALL + wall_from]).wait_recv()
                    leaving(index, half, dy, dc).wait_send()
    for send in sends:
        send.wait_send()

    @pl.when(first)
    def _():
        for index in range(len(CHUNKS)):
            for _, _, copy in passing(index):
                copy.wait_send()

    @pl.when((x == 1) | (x == 2))
    def _():
        arrival(end_land.at[3], end_sem.at[3]).wait_send()


def on_device(start_state, end_state, coupling, inverse_ops, mirror_rows, slab_steps):
    anywhere = pl.BlockSpec(memory_space=pl.ANY)
    start = start_state[0]
    arrived = pl.pallas_call(
        kernel,
        out_shape=jax.ShapeDtypeStruct((3, ROWS, WALL * LANES), F32),
        in_specs=[anywhere] * 4 + [pl.BlockSpec(memory_space=pltpu.VMEM), pl.BlockSpec(memory_space=pltpu.SMEM)],
        out_specs=anywhere,
        scratch_shapes=[
            pltpu.VMEM((3, NY + len(DETOUR) * ROWS, LANES), F32),
            pltpu.VMEM((4, NY, LANES), F32),
            pltpu.VMEM((3, NY, LANES), F32),
            pltpu.VMEM((3, NY, LANES), F32),
            pltpu.VMEM((3, NY, LANES), F32),
            pltpu.VMEM((2, NY, NY), F32),
            pltpu.VMEM((2 * NY, 3 * NY), BF16),
            pltpu.VMEM((3 * NY, 2 * LANES), BF16),
            pltpu.VMEM((NY, NY), BF16),
            pltpu.VMEM((NY, 2 * LANES), F32),
            pltpu.VMEM((3, NY, LANES), F32),
            pltpu.SemaphoreType.DMA((3,)),
            pltpu.SemaphoreType.DMA((4,)),
            pltpu.SemaphoreType.DMA((len(CHUNKS) * (WALL + len(DETOUR)),)),
            pltpu.SemaphoreType.DMA((4,)),
            pltpu.SemaphoreType.DMA((len(CHUNKS) * WALL,)),
            pltpu.SemaphoreType.DMA((len(CHUNKS),)),
        ],
        compiler_params=pltpu.CompilerParams(
            collective_id=0, has_side_effects=True, vmem_limit_bytes=40 * 1024 * 1024
        ),
        name="shooting",
    )(start, end_state[0], coupling[0], inverse_ops, mirror_rows.reshape(1, NY), slab_steps)
    return (arrived + start)[None]


def solution(mesh):
    in_specs = (
        P("tm", None, "wall", None),
        P("tm", None, None, "wall"),
        P("tm", None, None, "wall"),
        P("wall", None, None),
        P(),
        P("tm"),
    )
    out_specs = P("tm", None, "wall", None)
    return jax.shard_map(
        on_device, mesh=mesh, in_specs=in_specs, out_specs=out_specs, check_vma=False
    )
```

```python
import functools

import jax
import jax.numpy as jnp
from jax import lax
from jax.experimental import pallas as pl
from jax.experimental.pallas import tpu as pltpu
from jax.sharding import PartitionSpec as P

STEPS = 8
NY = 384
ROWS = 24
LANES = 128
WALL = 16
CHUNKS = ((0, 2), (2, 1))
OUTGOING = ((0, 1), (1, 2))
SLOTS = ((0, 1), (2, 1))
SIGN = (1.0, -1.0, 1.0)
DETOUR = ((0, 0), (0, 1), (1, 0))
MESH = pl.DeviceIdType.MESH
F32 = jnp.float32
BF16 = jnp.bfloat16


def place():
    tm = lax.axis_index("tm")
    wall = lax.axis_index("wall")
    x = lax.rem(tm, 4)
    y = lax.rem(lax.div(wall, 2), 4)
    core = lax.rem(wall, 2)
    z = lax.div(wall, 8) * 8 + lax.div(tm, 4)
    return x, y, z, core


def halves(value):
    high = value.astype(BF16)
    return high, (value - high.astype(F32)).astype(BF16)


def permuted(onehot, value):
    high = value.astype(BF16)
    rest = value - high.astype(F32)
    middle, low = halves(rest)
    dot = functools.partial(jnp.dot, preferred_element_type=F32)
    return (dot(onehot, high) + dot(onehot, middle)) + dot(onehot, low)


def lane_tile(rows):
    return lax.broadcasted_iota(jnp.int32, (rows, LANES), 1) < 64


def packed(zero, one, lower):
    return (jnp.where(lower, zero, pltpu.roll(one, 64, 1)),
            jnp.where(lower, pltpu.roll(zero, 64, 1), one))


def kernel(start_ref, end_ref, coupling_ref, ops_ref, mirror_ref, steps_ref, out_ref,
           rows_v, pack, land, end_land, end_send, end_v, coup_v, ops_v, mirror_v, wcat, xcat, onehot, state, shared,
           result, local_sem, send_sem, land_sem, end_sem, out_sem, own_sem):
    loads = [
        pltpu.make_async_copy(start_ref, rows_v, local_sem.at[0]),
        pltpu.make_async_copy(mirror_ref, mirror_v, local_sem.at[1]),
        pltpu.make_async_copy(end_ref, end_v, local_sem.at[2]),
        pltpu.make_async_copy(ops_ref, ops_v, local_sem.at[3]),
        pltpu.make_async_copy(coupling_ref, coup_v, local_sem.at[4]),
    ]
    for load in loads:
        load.start()

    x, y, z, core = place()
    tm, wall = lax.axis_index("tm"), lax.axis_index("wall")
    first = x == 0
    last = x == 3
    tm_before, tm_after = lax.rem(tm + 31, 32), lax.rem(tm + 1, 32)

    def upper(height):
        return lax.div(lax.rem(height, 16), 8) * 8

    def column(x_at, height):
        return lax.rem(height, 8) * 4 + x_at

    y_parts = [lax.rem(y + dy, 4) * 2 for dy in range(4)]
    core_parts = [core, 1 - core]
    here = y_parts[0] + core
    behind = jnp.where(first, 1, 0)
    ahead = jnp.where(last, 1, 0)
    halves_to = {half: upper(z + half + 16 - behind) for half in (8, 0)}
    halves_from = {half: upper(z + half + ahead) for half in (8, 0)}
    halves_in = {half: upper(z + half) for half in (8, 0)}
    next_run = lax.rem(lax.div(tm, 4) + 1, 8) * 4
    run_before = lax.rem(lax.div(tm, 4) + 7, 8) * 4

    barrier = pltpu.get_barrier_semaphore()

    def greet(*device):
        pl.semaphore_signal(barrier, inc=1, device_id=device, device_id_type=MESH)

    for other in range(WALL):
        greet(tm_after, other)
    greet(tm_before, wall)

    @pl.when(first)
    def _():
        for dy, dc in DETOUR:
            greet(column(0, z + 2), upper(z + 2) + y_parts[-dy] + core_parts[dc])
        greet(run_before + 1, wall)
        greet(run_before + 2, wall)

    @pl.when(last)
    def _():
        greet(column(0, z + 7), upper(z + 7) + here)

    @pl.when(x == 1)
    def _():
        greet(tm + 2, wall)

    loads[0].wait()
    narrow = lane_tile(ROWS)

    def pack_columns(number, carry):
        lanes = pl.ds(pl.multiple_of(number * LANES, LANES), LANES)
        pack[0, :, lanes], pack[2, :, lanes] = packed(rows_v[0, :, lanes], rows_v[1, :, lanes], narrow)
        pack[1, :, lanes] = rows_v[2, :, lanes]
        return carry

    lax.fori_loop(0, WALL, pack_columns, 0, unroll=4)
    pl.semaphore_wait(barrier, jnp.where(first, WALL + 5, WALL + 2))

    def first_hop(index, half, dy, dc):
        wall_to = halves_to[half] + y_parts[dy] + core_parts[dc]
        lanes = pl.multiple_of(wall_to * LANES, LANES)
        tm_to, row, sem = tm_before, wall * ROWS, index * WALL + wall
        comp, count = CHUNKS[index]
        if half and (dy, dc) in DETOUR:
            comp, count = 0, 3
            number = DETOUR.index((dy, dc))
            tm_to = jnp.where(first, column(0, z + 14), tm_to)
            wall_to = jnp.where(first, upper(z + 14) + y_parts[dy] + core_parts[dc], wall_to)
            row = jnp.where(first, NY + number * ROWS, row)
            sem = jnp.where(first, len(CHUNKS) * WALL + number, sem)
        return pltpu.make_async_remote_copy(
            pack.at[pl.ds(comp, count), :, pl.ds(lanes, LANES)],
            land.at[pl.ds(comp, count), pl.ds(pl.multiple_of(row, 8), ROWS), :],
            send_sem.at[index], land_sem.at[sem], device_id=(tm_to, wall_to), device_id_type=MESH)

    pairs = [(dy, dc) for dy in range(4) for dc in range(2)]
    plain = [(half, dy, dc) for half in (8, 0) for dy, dc in pairs if not half or (dy, dc) not in DETOUR]
    sends = [[first_hop(0, 8, dy, dc) for dy, dc in DETOUR] + [first_hop(0, *offset) for offset in plain]]
    sends += [[first_hop(index, *offset) for offset in plain] for index in range(1, len(CHUNKS))]
    for send in sends[0]:
        send.start()

    lower = lane_tile(NY)
    signs = [jnp.where(lower, SIGN[0], SIGN[1]), SIGN[2], jnp.where(lower, SIGN[0], SIGN[1])]
    source = lax.broadcasted_iota(jnp.int32, (NY, NY), 0)
    loads[1].wait()
    onehot[...] = jnp.where(source == mirror_v[...].reshape(1, NY), 1.0, 0.0).astype(BF16)
    loads[2].wait()
    kept = end_v[2]
    end_v[0], end_v[2] = packed(end_v[0], end_v[1], lower)
    end_v[1] = kept
    end_sends = []
    for comp in (1, 2, 0):
        end_send[comp] = permuted(onehot[...], end_v[comp]) * signs[comp]
        slot, tm_to = comp, tm_after
        if comp:
            tm_to = jnp.where(last, tm - (3 - comp), tm_to)
            slot = jnp.where(last, 3, comp)
        send = pltpu.make_async_remote_copy(
            end_send.at[comp], end_land.at[slot], send_sem.at[len(CHUNKS)], end_sem.at[slot],
            device_id=(tm_to, wall), device_id_type=MESH)
        send.start()
        end_sends.append(send)

    def arrival(ref, sem):
        return pltpu.make_async_remote_copy(
            ref, ref, send_sem.at[len(CHUNKS) + 1], sem, device_id=(tm, wall), device_id_type=MESH)

    def passing(number):
        dy, dc = DETOUR[number]
        wall_from = upper(z + 2) + y_parts[-dy] + core_parts[dc]
        held = land.at[:, pl.ds(NY + number * ROWS, ROWS), :]
        return held, pltpu.make_async_remote_copy(
            held, land.at[:, pl.ds(pl.multiple_of(wall_from * ROWS, 8), ROWS), :],
            send_sem.at[len(CHUNKS) + 1], land_sem.at[wall_from],
            device_id=(column(3, z + 9), upper(z + 9) + here), device_id_type=MESH)

    @pl.when(first)
    def _():
        for number in range(len(DETOUR)):
            held, copy = passing(number)
            arrival(held, land_sem.at[len(CHUNKS) * WALL + number]).wait_recv()
            copy.start()

    loads[3].wait()
    for group in range(2):
        high, low = halves(ops_v[group])
        wcat[group, :, 0:NY] = high
        wcat[group, :, NY:2 * NY] = low
        wcat[group, :, 2 * NY:3 * NY] = high
    loads[4].wait()
    kept = coup_v[2]
    coup_v[0], coup_v[2] = packed(coup_v[0], coup_v[1], lower)
    coup_v[1] = kept

    @pl.when((x == 1) | (x == 2))
    def _():
        arrival(end_land.at[3], end_sem.at[3]).wait_recv()
        pltpu.make_async_remote_copy(
            end_land.at[3], end_land.at[x], send_sem.at[len(CHUNKS) + 1], end_sem.at[x],
            device_id=(next_run, wall), device_id_type=MESH).start()

    for send in sends[0]:
        send.wait_send()
    for send in sends[1]:
        send.start()

    def leaving(index, half, dy, dc):
        comp, count = OUTGOING[index]
        wall_to = halves_in[half] + y_parts[dy] + core_parts[dc]
        return pltpu.make_async_remote_copy(
            result.at[pl.ds(comp, count), pl.ds(pl.multiple_of(wall_to * ROWS, 8), ROWS), :],
            out_ref.at[pl.ds(comp, count), :, pl.ds(pl.multiple_of(wall * LANES, LANES), LANES)],
            send_sem.at[len(CHUNKS) + 2], out_sem.at[index * WALL + wall], device_id=(tm, wall_to), device_id_type=MESH)

    def staying(index):
        comp, count = OUTGOING[index]
        return pltpu.make_async_copy(
            result.at[pl.ds(comp, count), pl.ds(pl.multiple_of(wall * ROWS, 8), ROWS), :],
            out_ref.at[pl.ds(comp, count), :, pl.ds(pl.multiple_of(wall * LANES, LANES), LANES)],
            own_sem.at[index])

    steps = steps_ref[0]
    others = [(half, dy, dc) for half in (8, 0) for dy, dc in pairs if half or dy or dc]
    for index, (comp, count) in enumerate(CHUNKS):
        def landed(half, dy, dc, comp, count):
            wall_from = halves_from[half] + y_parts[-dy] + core_parts[dc]
            arrival(land.at[pl.ds(comp, count), pl.ds(pl.multiple_of(wall_from * ROWS, 8), ROWS), :],
                    land_sem.at[index * WALL + wall_from]).wait_recv()

        if index == 0:
            for dy, dc in DETOUR:
                landed(8, dy, dc, 0, 3)
        for offset in plain:
            landed(*offset, comp, count)
        if 1 < index + 2 < len(CHUNKS):
            for send in sends[index + 2]:
                send.start()
        fresh = SLOTS[index] if not index else SLOTS[index][:1]
        for at, slot in enumerate(SLOTS[index]):
            lanes = slice(at * LANES, (at + 1) * LANES)
            if slot in fresh:
                state[:, lanes] = end_v[slot] - permuted(onehot[...], land[slot, 0:NY, :]) * signs[slot]
                if slot == 1:
                    shared[0] = state[:, lanes]
            else:
                state[:, lanes] = shared[0]

        def step(number, carry, index=index):
            for at, slot in enumerate(SLOTS[index]):
                lanes = slice(at * LANES, (at + 1) * LANES)
                high, low = halves(coup_v[slot] * state[:, lanes])
                xcat[0:NY, lanes] = high
                xcat[NY:2 * NY, lanes] = high
                xcat[2 * NY:3 * NY, lanes] = low
            advanced = jnp.dot(wcat[index], xcat[...], preferred_element_type=F32)
            state[...] = jnp.where(number < steps, advanced, state[...])
            return carry

        lax.fori_loop(0, STEPS, step, 0)
        leave, many = OUTGOING[index]
        for slot in range(leave, leave + many):
            arrival(end_land.at[slot], end_sem.at[slot]).wait_recv()
            if slot == 1:
                value = jnp.where(lower, shared[1], state[:, LANES:])
            else:
                value = state[:, 0:LANES]
            result[slot] = value - end_land[slot]
        if not index:
            shared[1] = state[:, LANES:]
        for offset in others:
            leaving(index, *offset).start()
        staying(index).start()

    for index, (comp, count) in enumerate(OUTGOING):
        staying(index).wait()
        for half, dy, dc in others:
            wall_from = halves_in[half] + y_parts[dy] + core_parts[dc]
            arrival(out_ref.at[pl.ds(comp, count), :, pl.ds(pl.multiple_of(wall_from * LANES, LANES), LANES)],
                    out_sem.at[index * WALL + wall_from]).wait_recv()
            leaving(index, half, dy, dc).wait_send()
    for send in sum(sends[1:], end_sends):
        send.wait_send()

    @pl.when(first)
    def _():
        for number in range(len(DETOUR)):
            passing(number)[1].wait_send()

    @pl.when((x == 1) | (x == 2))
    def _():
        arrival(end_land.at[3], end_sem.at[3]).wait_send()


def finish(arrived_ref, start_ref, out_ref):
    lower = lane_tile(ROWS)
    for at in range(0, arrived_ref.shape[2], LANES):
        lanes = slice(at, at + LANES)
        zero, one = packed(arrived_ref[0, :, lanes], arrived_ref[2, :, lanes], lower)
        out_ref[0, :, lanes] = zero + start_ref[0, :, lanes]
        out_ref[1, :, lanes] = one + start_ref[1, :, lanes]
        out_ref[2, :, lanes] = arrived_ref[1, :, lanes] + start_ref[2, :, lanes]


def on_device(start_state, end_state, coupling, inverse_ops, mirror_rows, slab_steps):
    anywhere = pl.BlockSpec(memory_space=pl.ANY)
    start = start_state[0]
    arrived = pl.pallas_call(
        kernel,
        out_shape=jax.ShapeDtypeStruct((3, ROWS, WALL * LANES), F32),
        in_specs=[anywhere] * 5 + [pl.BlockSpec(memory_space=pltpu.SMEM)],
        out_specs=anywhere,
        scratch_shapes=[
            pltpu.VMEM((3, ROWS, WALL * LANES), F32),
            pltpu.VMEM((3, ROWS, WALL * LANES), F32),
            pltpu.VMEM((3, NY + len(DETOUR) * ROWS, LANES), F32),
            pltpu.VMEM((4, NY, LANES), F32),
            pltpu.VMEM((3, NY, LANES), F32),
            pltpu.VMEM((3, NY, LANES), F32),
            pltpu.VMEM((3, NY, LANES), F32),
            pltpu.VMEM((2, NY, NY), F32),
            pltpu.VMEM((NY,), jnp.int32),
            pltpu.VMEM((2, NY, 3 * NY), BF16),
            pltpu.VMEM((3 * NY, 2 * LANES), BF16),
            pltpu.VMEM((NY, NY), BF16),
            pltpu.VMEM((NY, 2 * LANES), F32),
            pltpu.VMEM((2, NY, LANES), F32),
            pltpu.VMEM((3, NY, LANES), F32),
            pltpu.SemaphoreType.DMA((5,)),
            pltpu.SemaphoreType.DMA((len(CHUNKS) + 3,)),
            pltpu.SemaphoreType.DMA((len(CHUNKS) * WALL + len(DETOUR),)),
            pltpu.SemaphoreType.DMA((4,)),
            pltpu.SemaphoreType.DMA((len(CHUNKS) * WALL,)),
            pltpu.SemaphoreType.DMA((len(CHUNKS),)),
        ],
        compiler_params=pltpu.CompilerParams(
            collective_id=0, has_side_effects=True, vmem_limit_bytes=60 * 1024 * 1024
        ),
        name="shooting",
    )(start, end_state[0], coupling[0], inverse_ops, mirror_rows, slab_steps)
    block = pl.BlockSpec((3, ROWS, 4 * LANES), lambda at: (0, 0, at))
    gradient = pl.pallas_call(
        finish,
        out_shape=jax.ShapeDtypeStruct((3, ROWS, WALL * LANES), F32),
        grid=(WALL // 4,),
        in_specs=[block, block],
        out_specs=block,
        name="finish",
    )(arrived, start)
    return gradient[None]


def solution(mesh):
    in_specs = (
        P("tm", None, "wall", None),
        P("tm", None, None, "wall"),
        P("tm", None, None, "wall"),
        P("wall", None, None),
        P(),
        P("tm"),
    )
    out_specs = P("tm", None, "wall", None)
    return jax.shard_map(
        on_device, mesh=mesh, in_specs=in_specs, out_specs=out_specs, check_vma=False
    )
```

```python
import functools

import jax
import jax.numpy as jnp
from jax import lax
from jax.experimental import pallas as pl
from jax.experimental.pallas import tpu as pltpu
from jax.sharding import PartitionSpec as P

STEPS = 8
NY = 384
ROWS = 24
LANES = 128
WALL = 16
CHUNKS = ((0, 2), (2, 1))
OUTGOING = ((0, 1), (1, 2))
SLOTS = ((0, 1), (2, 1))
SIGN = (1.0, -1.0, 1.0)
DETOUR = ((0, 0), (0, 1), (1, 0))
MESH = pl.DeviceIdType.MESH
F32 = jnp.float32
BF16 = jnp.bfloat16


def place():
    tm = lax.axis_index("tm")
    wall = lax.axis_index("wall")
    x = lax.rem(tm, 4)
    y = lax.rem(lax.div(wall, 2), 4)
    core = lax.rem(wall, 2)
    z = lax.div(wall, 8) * 8 + lax.div(tm, 4)
    return x, y, z, core


def halves(value):
    high = value.astype(BF16)
    return high, (value - high.astype(F32)).astype(BF16)


def permuted(onehot, value):
    high = value.astype(BF16)
    rest = value - high.astype(F32)
    middle, low = halves(rest)
    dot = functools.partial(jnp.dot, preferred_element_type=F32)
    return (dot(onehot, high) + dot(onehot, middle)) + dot(onehot, low)


def lane_tile(rows):
    return lax.broadcasted_iota(jnp.int32, (rows, LANES), 1) < 64


def packed(zero, one, lower):
    return (jnp.where(lower, zero, pltpu.roll(one, 64, 1)),
            jnp.where(lower, pltpu.roll(zero, 64, 1), one))


def kernel(start_ref, end_ref, coupling_ref, ops_ref, mirror_ref, steps_ref, out_ref,
           rows_v, pack, land, end_land, end_send, end_v, coup_v, ops_v, mirror_v, wcat, xcat, onehot, state, shared,
           result, local_sem, send_sem, land_sem, end_sem, out_sem, own_sem):
    loads = [
        pltpu.make_async_copy(start_ref, rows_v, local_sem.at[0]),
        pltpu.make_async_copy(mirror_ref, mirror_v, local_sem.at[1]),
        pltpu.make_async_copy(end_ref, end_v, local_sem.at[2]),
        pltpu.make_async_copy(ops_ref, ops_v, local_sem.at[3]),
        pltpu.make_async_copy(coupling_ref, coup_v, local_sem.at[4]),
    ]
    for load in loads:
        load.start()

    x, y, z, core = place()
    tm, wall = lax.axis_index("tm"), lax.axis_index("wall")
    first = x == 0
    last = x == 3
    tm_before, tm_after = lax.rem(tm + 31, 32), lax.rem(tm + 1, 32)

    def upper(height):
        return lax.div(lax.rem(height, 16), 8) * 8

    def column(x_at, height):
        return lax.rem(height, 8) * 4 + x_at

    y_parts = [lax.rem(y + dy, 4) * 2 for dy in range(4)]
    core_parts = [core, 1 - core]
    here = y_parts[0] + core
    behind = jnp.where(first, 1, 0)
    ahead = jnp.where(last, 1, 0)
    halves_to = {half: upper(z + half + 16 - behind) for half in (8, 0)}
    halves_from = {half: upper(z + half + ahead) for half in (8, 0)}
    halves_in = {half: upper(z + half) for half in (8, 0)}
    next_run = lax.rem(lax.div(tm, 4) + 1, 8) * 4
    run_before = lax.rem(lax.div(tm, 4) + 7, 8) * 4

    barrier = pltpu.get_barrier_semaphore()

    def greet(*device):
        pl.semaphore_signal(barrier, inc=1, device_id=device, device_id_type=MESH)

    for other in range(WALL):
        greet(tm_after, other)
    greet(tm_before, wall)

    @pl.when(first)
    def _():
        for dy, dc in DETOUR:
            greet(column(0, z + 2), upper(z + 2) + y_parts[-dy] + core_parts[dc])
        greet(run_before + 1, wall)
        greet(run_before + 2, wall)

    @pl.when(last)
    def _():
        greet(column(0, z + 7), upper(z + 7) + here)

    @pl.when(x == 1)
    def _():
        greet(tm + 2, wall)

    loads[0].wait()
    narrow = lane_tile(ROWS)

    def pack_columns(number, carry):
        lanes = pl.ds(pl.multiple_of(number * LANES, LANES), LANES)
        pack[0, :, lanes], pack[2, :, lanes] = packed(rows_v[0, :, lanes], rows_v[1, :, lanes], narrow)
        pack[1, :, lanes] = rows_v[2, :, lanes]
        return carry

    lax.fori_loop(0, WALL, pack_columns, 0, unroll=4)
    pl.semaphore_wait(barrier, jnp.where(first, WALL + 5, WALL + 2))

    def first_hop(index, half, dy, dc):
        wall_to = halves_to[half] + y_parts[dy] + core_parts[dc]
        lanes = pl.multiple_of(wall_to * LANES, LANES)
        tm_to, row, sem = tm_before, wall * ROWS, index * WALL + wall
        comp, count = CHUNKS[index]
        if half and (dy, dc) in DETOUR:
            comp, count = 0, 3
            number = DETOUR.index((dy, dc))
            tm_to = jnp.where(first, column(0, z + 14), tm_to)
            wall_to = jnp.where(first, upper(z + 14) + y_parts[dy] + core_parts[dc], wall_to)
            row = jnp.where(first, NY + number * ROWS, row)
            sem = jnp.where(first, len(CHUNKS) * WALL + number, sem)
        return pltpu.make_async_remote_copy(
            pack.at[pl.ds(comp, count), :, pl.ds(lanes, LANES)],
            land.at[pl.ds(comp, count), pl.ds(pl.multiple_of(row, 8), ROWS), :],
            send_sem.at[index], land_sem.at[sem], device_id=(tm_to, wall_to), device_id_type=MESH)

    pairs = [(dy, dc) for dy in range(4) for dc in range(2)]
    plain = [(half, dy, dc) for half in (8, 0) for dy, dc in pairs if not half or (dy, dc) not in DETOUR]
    sends = [[first_hop(0, 8, dy, dc) for dy, dc in DETOUR] + [first_hop(0, *offset) for offset in plain]]
    sends += [[first_hop(index, *offset) for offset in plain] for index in range(1, len(CHUNKS))]
    for send in sends[0]:
        send.start()

    lower = lane_tile(NY)
    signs = [jnp.where(lower, SIGN[0], SIGN[1]), SIGN[2], jnp.where(lower, SIGN[0], SIGN[1])]
    source = lax.broadcasted_iota(jnp.int32, (NY, NY), 0)
    loads[1].wait()
    onehot[...] = jnp.where(source == mirror_v[...].reshape(1, NY), 1.0, 0.0).astype(BF16)
    loads[2].wait()
    kept = end_v[2]
    end_v[0], end_v[2] = packed(end_v[0], end_v[1], lower)
    end_v[1] = kept
    end_sends = []
    for comp in (1, 2, 0):
        end_send[comp] = permuted(onehot[...], end_v[comp]) * signs[comp]
        slot, tm_to = comp, tm_after
        if comp:
            tm_to = jnp.where(last, tm - (3 - comp), tm_to)
            slot = jnp.where(last, 3, comp)
        send = pltpu.make_async_remote_copy(
            end_send.at[comp], end_land.at[slot], send_sem.at[len(CHUNKS)], end_sem.at[slot],
            device_id=(tm_to, wall), device_id_type=MESH)
        send.start()
        end_sends.append(send)

    def arrival(ref, sem):
        return pltpu.make_async_remote_copy(
            ref, ref, send_sem.at[len(CHUNKS) + 1], sem, device_id=(tm, wall), device_id_type=MESH)

    def passing(number):
        dy, dc = DETOUR[number]
        wall_from = upper(z + 2) + y_parts[-dy] + core_parts[dc]
        held = land.at[:, pl.ds(NY + number * ROWS, ROWS), :]
        return held, pltpu.make_async_remote_copy(
            held, land.at[:, pl.ds(pl.multiple_of(wall_from * ROWS, 8), ROWS), :],
            send_sem.at[len(CHUNKS) + 1], land_sem.at[wall_from],
            device_id=(column(3, z + 9), upper(z + 9) + here), device_id_type=MESH)

    @pl.when(first)
    def _():
        for number in range(len(DETOUR)):
            held, copy = passing(number)
            arrival(held, land_sem.at[len(CHUNKS) * WALL + number]).wait_recv()
            copy.start()

    loads[3].wait()
    for group in range(2):
        high, low = halves(ops_v[group])
        wcat[group, :, 0:NY] = high
        wcat[group, :, NY:2 * NY] = low
        wcat[group, :, 2 * NY:3 * NY] = high
    loads[4].wait()
    kept = coup_v[2]
    coup_v[0], coup_v[2] = packed(coup_v[0], coup_v[1], lower)
    coup_v[1] = kept

    for send in sends[1]:
        send.start()

    @pl.when((x == 1) | (x == 2))
    def _():
        arrival(end_land.at[3], end_sem.at[3]).wait_recv()
        pltpu.make_async_remote_copy(
            end_land.at[3], end_land.at[x], send_sem.at[len(CHUNKS) + 1], end_sem.at[x],
            device_id=(next_run, wall), device_id_type=MESH).start()


    def leaving(index, half, dy, dc):
        comp, count = OUTGOING[index]
        wall_to = halves_in[half] + y_parts[dy] + core_parts[dc]
        return pltpu.make_async_remote_copy(
            result.at[pl.ds(comp, count), pl.ds(pl.multiple_of(wall_to * ROWS, 8), ROWS), :],
            out_ref.at[pl.ds(comp, count), :, pl.ds(pl.multiple_of(wall * LANES, LANES), LANES)],
            send_sem.at[len(CHUNKS) + 2], out_sem.at[index * WALL + wall], device_id=(tm, wall_to), device_id_type=MESH)

    def staying(index):
        comp, count = OUTGOING[index]
        return pltpu.make_async_copy(
            result.at[pl.ds(comp, count), pl.ds(pl.multiple_of(wall * ROWS, 8), ROWS), :],
            out_ref.at[pl.ds(comp, count), :, pl.ds(pl.multiple_of(wall * LANES, LANES), LANES)],
            own_sem.at[index])

    steps = steps_ref[0]
    others = [(half, dy, dc) for half in (8, 0) for dy, dc in pairs if half or dy or dc]
    for index, (comp, count) in enumerate(CHUNKS):
        def landed(half, dy, dc, comp, count):
            wall_from = halves_from[half] + y_parts[-dy] + core_parts[dc]
            arrival(land.at[pl.ds(comp, count), pl.ds(pl.multiple_of(wall_from * ROWS, 8), ROWS), :],
                    land_sem.at[index * WALL + wall_from]).wait_recv()

        if index == 0:
            for dy, dc in DETOUR:
                landed(8, dy, dc, 0, 3)
        for offset in plain:
            landed(*offset, comp, count)
        if 1 < index + 2 < len(CHUNKS):
            for send in sends[index + 2]:
                send.start()
        fresh = SLOTS[index] if not index else SLOTS[index][:1]
        for at, slot in enumerate(SLOTS[index]):
            lanes = slice(at * LANES, (at + 1) * LANES)
            if slot in fresh:
                state[:, lanes] = end_v[slot] - permuted(onehot[...], land[slot, 0:NY, :]) * signs[slot]
                if slot == 1:
                    shared[0] = state[:, lanes]
            else:
                state[:, lanes] = shared[0]

        def step(number, carry, index=index):
            for at, slot in enumerate(SLOTS[index]):
                lanes = slice(at * LANES, (at + 1) * LANES)
                high, low = halves(coup_v[slot] * state[:, lanes])
                xcat[0:NY, lanes] = high
                xcat[NY:2 * NY, lanes] = high
                xcat[2 * NY:3 * NY, lanes] = low
            advanced = jnp.dot(wcat[index], xcat[...], preferred_element_type=F32)
            state[...] = jnp.where(number < steps, advanced, state[...])
            return carry

        lax.fori_loop(0, STEPS, step, 0)
        leave, many = OUTGOING[index]
        for slot in range(leave, leave + many):
            arrival(end_land.at[slot], end_sem.at[slot]).wait_recv()
            if slot == 1:
                value = jnp.where(lower, shared[1], state[:, LANES:])
            else:
                value = state[:, 0:LANES]
            result[slot] = value - end_land[slot]
        if not index:
            shared[1] = state[:, LANES:]
        for offset in others:
            leaving(index, *offset).start()
        staying(index).start()

    for index, (comp, count) in enumerate(OUTGOING):
        staying(index).wait()
        for half, dy, dc in others:
            wall_from = halves_in[half] + y_parts[dy] + core_parts[dc]
            arrival(out_ref.at[pl.ds(comp, count), :, pl.ds(pl.multiple_of(wall_from * LANES, LANES), LANES)],
                    out_sem.at[index * WALL + wall_from]).wait_recv()
            leaving(index, half, dy, dc).wait_send()
    for send in sum(sends, end_sends):
        send.wait_send()

    @pl.when(first)
    def _():
        for number in range(len(DETOUR)):
            passing(number)[1].wait_send()

    @pl.when((x == 1) | (x == 2))
    def _():
        arrival(end_land.at[3], end_sem.at[3]).wait_send()


def finish(arrived_ref, start_ref, out_ref):
    lower = lane_tile(ROWS)
    for at in range(0, arrived_ref.shape[2], LANES):
        lanes = slice(at, at + LANES)
        zero, one = packed(arrived_ref[0, :, lanes], arrived_ref[2, :, lanes], lower)
        out_ref[0, :, lanes] = zero + start_ref[0, :, lanes]
        out_ref[1, :, lanes] = one + start_ref[1, :, lanes]
        out_ref[2, :, lanes] = arrived_ref[1, :, lanes] + start_ref[2, :, lanes]


def on_device(start_state, end_state, coupling, inverse_ops, mirror_rows, slab_steps):
    anywhere = pl.BlockSpec(memory_space=pl.ANY)
    start = start_state[0]
    arrived = pl.pallas_call(
        kernel,
        out_shape=jax.ShapeDtypeStruct((3, ROWS, WALL * LANES), F32),
        in_specs=[anywhere] * 5 + [pl.BlockSpec(memory_space=pltpu.SMEM)],
        out_specs=anywhere,
        scratch_shapes=[
            pltpu.VMEM((3, ROWS, WALL * LANES), F32),
            pltpu.VMEM((3, ROWS, WALL * LANES), F32),
            pltpu.VMEM((3, NY + len(DETOUR) * ROWS, LANES), F32),
            pltpu.VMEM((4, NY, LANES), F32),
            pltpu.VMEM((3, NY, LANES), F32),
            pltpu.VMEM((3, NY, LANES), F32),
            pltpu.VMEM((3, NY, LANES), F32),
            pltpu.VMEM((2, NY, NY), F32),
            pltpu.VMEM((NY,), jnp.int32),
            pltpu.VMEM((2, NY, 3 * NY), BF16),
            pltpu.VMEM((3 * NY, 2 * LANES), BF16),
            pltpu.VMEM((NY, NY), BF16),
            pltpu.VMEM((NY, 2 * LANES), F32),
            pltpu.VMEM((2, NY, LANES), F32),
            pltpu.VMEM((3, NY, LANES), F32),
            pltpu.SemaphoreType.DMA((5,)),
            pltpu.SemaphoreType.DMA((len(CHUNKS) + 3,)),
            pltpu.SemaphoreType.DMA((len(CHUNKS) * WALL + len(DETOUR),)),
            pltpu.SemaphoreType.DMA((4,)),
            pltpu.SemaphoreType.DMA((len(CHUNKS) * WALL,)),
            pltpu.SemaphoreType.DMA((len(CHUNKS),)),
        ],
        compiler_params=pltpu.CompilerParams(
            collective_id=0, has_side_effects=True, vmem_limit_bytes=60 * 1024 * 1024
        ),
        name="shooting",
    )(start, end_state[0], coupling[0], inverse_ops, mirror_rows, slab_steps)
    block = pl.BlockSpec((3, ROWS, 8 * LANES), lambda at: (0, 0, at))
    gradient = pl.pallas_call(
        finish,
        out_shape=jax.ShapeDtypeStruct((3, ROWS, WALL * LANES), F32),
        grid=(2,),
        in_specs=[block, block],
        out_specs=block,
        name="finish",
    )(arrived, start)
    return gradient[None]


def solution(mesh):
    in_specs = (
        P("tm", None, "wall", None),
        P("tm", None, None, "wall"),
        P("tm", None, None, "wall"),
        P("wall", None, None),
        P(),
        P("tm"),
    )
    out_specs = P("tm", None, "wall", None)
    return jax.shard_map(
        on_device, mesh=mesh, in_specs=in_specs, out_specs=out_specs, check_vma=False
    )
```

```python
import functools

import jax
import jax.numpy as jnp
from jax import lax
from jax.experimental import pallas as pl
from jax.experimental.pallas import tpu as pltpu
from jax.sharding import PartitionSpec as P

STEPS = 8
NY = 384
ROWS = 24
LANES = 128
WALL = 16
CHUNKS = ((0, 2), (2, 1))
OUTGOING = ((0, 1), (1, 2))
SLOTS = ((0, 1), (2, 1))
SIGN = (1.0, -1.0, 1.0)
DETOUR = ((0, 0), (0, 1), (1, 0))
MESH = pl.DeviceIdType.MESH
F32 = jnp.float32
BF16 = jnp.bfloat16


def place():
    tm = lax.axis_index("tm")
    wall = lax.axis_index("wall")
    x = lax.rem(tm, 4)
    y = lax.rem(lax.div(wall, 2), 4)
    core = lax.rem(wall, 2)
    z = lax.div(wall, 8) * 8 + lax.div(tm, 4)
    return x, y, z, core


def halves(value):
    high = value.astype(BF16)
    return high, (value - high.astype(F32)).astype(BF16)


def permuted(onehot, value):
    high = value.astype(BF16)
    rest = value - high.astype(F32)
    middle, low = halves(rest)
    dot = functools.partial(jnp.dot, preferred_element_type=F32)
    return (dot(onehot, high) + dot(onehot, middle)) + dot(onehot, low)


def lane_tile(rows):
    return lax.broadcasted_iota(jnp.int32, (rows, LANES), 1) < 64


def packed(zero, one, lower):
    return (jnp.where(lower, zero, pltpu.roll(one, 64, 1)),
            jnp.where(lower, pltpu.roll(zero, 64, 1), one))


def kernel(start_ref, end_ref, coupling_ref, ops_ref, mirror_ref, steps_ref, out_ref,
           rows_v, pack, land, end_land, end_send, end_v, coup_v, ops_v, mirror_v, wcat, xcat, onehot, state, shared,
           result, local_sem, send_sem, land_sem, end_sem, out_sem, own_sem, go_sem):
    loads = [
        pltpu.make_async_copy(start_ref, rows_v, local_sem.at[0]),
        pltpu.make_async_copy(mirror_ref, mirror_v, local_sem.at[1]),
        pltpu.make_async_copy(end_ref, end_v, local_sem.at[2]),
        pltpu.make_async_copy(ops_ref, ops_v, local_sem.at[3]),
        pltpu.make_async_copy(coupling_ref, coup_v, local_sem.at[4]),
    ]
    for load in loads:
        load.start()

    x, y, z, core = place()
    tm, wall = lax.axis_index("tm"), lax.axis_index("wall")
    first = x == 0
    last = x == 3
    tm_before, tm_after = lax.rem(tm + 31, 32), lax.rem(tm + 1, 32)

    def upper(height):
        return lax.div(lax.rem(height, 16), 8) * 8

    def column(x_at, height):
        return lax.rem(height, 8) * 4 + x_at

    y_parts = [lax.rem(y + dy, 4) * 2 for dy in range(4)]
    core_parts = [core, 1 - core]
    here = y_parts[0] + core
    behind = jnp.where(first, 1, 0)
    ahead = jnp.where(last, 1, 0)
    halves_to = {half: upper(z + half + 16 - behind) for half in (8, 0)}
    halves_from = {half: upper(z + half + ahead) for half in (8, 0)}
    halves_in = {half: upper(z + half) for half in (8, 0)}
    next_run = lax.rem(lax.div(tm, 4) + 1, 8) * 4
    run_before = lax.rem(lax.div(tm, 4) + 7, 8) * 4

    turns = x == 1
    leads = turns & (lax.div(tm_before, 4) < 4)
    trails = turns & (lax.div(tm_before, 4) >= 4)
    partner = lax.rem(tm + 16, 32)

    barrier = pltpu.get_barrier_semaphore()

    def greet(*device):
        pl.semaphore_signal(barrier, inc=1, device_id=device, device_id_type=MESH)

    for other in range(WALL):
        greet(tm_after, other)
    greet(tm_before, wall)

    @pl.when(trails)
    def _():
        greet(partner, wall)

    @pl.when(first)
    def _():
        for dy, dc in DETOUR:
            greet(column(0, z + 2), upper(z + 2) + y_parts[-dy] + core_parts[dc])
        greet(run_before + 1, wall)
        greet(run_before + 2, wall)

    @pl.when(last)
    def _():
        greet(column(0, z + 7), upper(z + 7) + here)

    @pl.when(x == 1)
    def _():
        greet(tm + 2, wall)

    loads[0].wait()
    narrow = lane_tile(ROWS)

    def pack_columns(number, carry):
        lanes = pl.ds(pl.multiple_of(number * LANES, LANES), LANES)
        pack[0, :, lanes], pack[2, :, lanes] = packed(rows_v[0, :, lanes], rows_v[1, :, lanes], narrow)
        pack[1, :, lanes] = rows_v[2, :, lanes]
        return carry

    lax.fori_loop(0, WALL, pack_columns, 0, unroll=4)
    pl.semaphore_wait(barrier, jnp.where(first, WALL + 5, WALL + 2) + jnp.where(leads, 1, 0))

    def first_hop(index, half, dy, dc):
        wall_to = halves_to[half] + y_parts[dy] + core_parts[dc]
        lanes = pl.multiple_of(wall_to * LANES, LANES)
        tm_to, row, sem = tm_before, wall * ROWS, index * WALL + wall
        comp, count = CHUNKS[index]
        if half and (dy, dc) in DETOUR:
            comp, count = 0, 3
            number = DETOUR.index((dy, dc))
            tm_to = jnp.where(first, column(0, z + 14), tm_to)
            wall_to = jnp.where(first, upper(z + 14) + y_parts[dy] + core_parts[dc], wall_to)
            row = jnp.where(first, NY + number * ROWS, row)
            sem = jnp.where(first, len(CHUNKS) * WALL + number, sem)
        return pltpu.make_async_remote_copy(
            pack.at[pl.ds(comp, count), :, pl.ds(lanes, LANES)],
            land.at[pl.ds(comp, count), pl.ds(pl.multiple_of(row, 8), ROWS), :],
            send_sem.at[index], land_sem.at[sem], device_id=(tm_to, wall_to), device_id_type=MESH)

    pairs = [(dy, dc) for dy in range(4) for dc in range(2)]
    plain = [(half, dy, dc) for half in (8, 0) for dy, dc in pairs if not half or (dy, dc) not in DETOUR]
    sends = [[first_hop(0, 8, dy, dc) for dy, dc in DETOUR] + [first_hop(0, *offset) for offset in plain]]
    sends += [[first_hop(index, *offset) for offset in plain] for index in range(1, len(CHUNKS))]
    @pl.when(trails)
    def _():
        pl.semaphore_wait(go_sem, 1)

    for send in sends[0]:
        send.start()

    @pl.when(leads)
    def _():
        pl.semaphore_signal(go_sem, inc=1, device_id=(partner, wall), device_id_type=MESH)

    lower = lane_tile(NY)
    signs = [jnp.where(lower, SIGN[0], SIGN[1]), SIGN[2], jnp.where(lower, SIGN[0], SIGN[1])]
    source = lax.broadcasted_iota(jnp.int32, (NY, NY), 0)
    loads[1].wait()
    onehot[...] = jnp.where(source == mirror_v[...].reshape(1, NY), 1.0, 0.0).astype(BF16)
    loads[2].wait()
    kept = end_v[2]
    end_v[0], end_v[2] = packed(end_v[0], end_v[1], lower)
    end_v[1] = kept
    end_sends = []
    for comp in (1, 2, 0):
        end_send[comp] = permuted(onehot[...], end_v[comp]) * signs[comp]
        slot, tm_to = comp, tm_after
        if comp:
            tm_to = jnp.where(last, tm - (3 - comp), tm_to)
            slot = jnp.where(last, 3, comp)
        send = pltpu.make_async_remote_copy(
            end_send.at[comp], end_land.at[slot], send_sem.at[len(CHUNKS)], end_sem.at[slot],
            device_id=(tm_to, wall), device_id_type=MESH)
        send.start()
        end_sends.append(send)

    def arrival(ref, sem):
        return pltpu.make_async_remote_copy(
            ref, ref, send_sem.at[len(CHUNKS) + 1], sem, device_id=(tm, wall), device_id_type=MESH)

    def passing(number):
        dy, dc = DETOUR[number]
        wall_from = upper(z + 2) + y_parts[-dy] + core_parts[dc]
        held = land.at[:, pl.ds(NY + number * ROWS, ROWS), :]
        return held, pltpu.make_async_remote_copy(
            held, land.at[:, pl.ds(pl.multiple_of(wall_from * ROWS, 8), ROWS), :],
            send_sem.at[len(CHUNKS) + 1], land_sem.at[wall_from],
            device_id=(column(3, z + 9), upper(z + 9) + here), device_id_type=MESH)

    @pl.when(first)
    def _():
        for number in range(len(DETOUR)):
            held, copy = passing(number)
            arrival(held, land_sem.at[len(CHUNKS) * WALL + number]).wait_recv()
            copy.start()

    loads[3].wait()
    for group in range(2):
        high, low = halves(ops_v[group])
        wcat[group, :, 0:NY] = high
        wcat[group, :, NY:2 * NY] = low
        wcat[group, :, 2 * NY:3 * NY] = high
    loads[4].wait()
    kept = coup_v[2]
    coup_v[0], coup_v[2] = packed(coup_v[0], coup_v[1], lower)
    coup_v[1] = kept

    for send in sends[1]:
        send.start()

    @pl.when((x == 1) | (x == 2))
    def _():
        arrival(end_land.at[3], end_sem.at[3]).wait_recv()
        pltpu.make_async_remote_copy(
            end_land.at[3], end_land.at[x], send_sem.at[len(CHUNKS) + 1], end_sem.at[x],
            device_id=(next_run, wall), device_id_type=MESH).start()


    def leaving(index, half, dy, dc):
        comp, count = OUTGOING[index]
        wall_to = halves_in[half] + y_parts[dy] + core_parts[dc]
        return pltpu.make_async_remote_copy(
            result.at[pl.ds(comp, count), pl.ds(pl.multiple_of(wall_to * ROWS, 8), ROWS), :],
            out_ref.at[pl.ds(comp, count), :, pl.ds(pl.multiple_of(wall * LANES, LANES), LANES)],
            send_sem.at[len(CHUNKS) + 2], out_sem.at[index * WALL + wall], device_id=(tm, wall_to), device_id_type=MESH)

    def staying(index):
        comp, count = OUTGOING[index]
        return pltpu.make_async_copy(
            result.at[pl.ds(comp, count), pl.ds(pl.multiple_of(wall * ROWS, 8), ROWS), :],
            out_ref.at[pl.ds(comp, count), :, pl.ds(pl.multiple_of(wall * LANES, LANES), LANES)],
            own_sem.at[index])

    steps = steps_ref[0]
    others = [(half, dy, dc) for half in (8, 0) for dy, dc in pairs if half or dy or dc]
    for index, (comp, count) in enumerate(CHUNKS):
        def landed(half, dy, dc, comp, count):
            wall_from = halves_from[half] + y_parts[-dy] + core_parts[dc]
            arrival(land.at[pl.ds(comp, count), pl.ds(pl.multiple_of(wall_from * ROWS, 8), ROWS), :],
                    land_sem.at[index * WALL + wall_from]).wait_recv()

        if index == 0:
            for dy, dc in DETOUR:
                landed(8, dy, dc, 0, 3)
        for offset in plain:
            landed(*offset, comp, count)
        if 1 < index + 2 < len(CHUNKS):
            for send in sends[index + 2]:
                send.start()
        fresh = SLOTS[index] if not index else SLOTS[index][:1]
        for at, slot in enumerate(SLOTS[index]):
            lanes = slice(at * LANES, (at + 1) * LANES)
            if slot in fresh:
                state[:, lanes] = end_v[slot] - permuted(onehot[...], land[slot, 0:NY, :]) * signs[slot]
                if slot == 1:
                    shared[0] = state[:, lanes]
            else:
                state[:, lanes] = shared[0]

        def step(number, carry, index=index):
            for at, slot in enumerate(SLOTS[index]):
                lanes = slice(at * LANES, (at + 1) * LANES)
                high, low = halves(coup_v[slot] * state[:, lanes])
                xcat[0:NY, lanes] = high
                xcat[NY:2 * NY, lanes] = high
                xcat[2 * NY:3 * NY, lanes] = low
            advanced = jnp.dot(wcat[index], xcat[...], preferred_element_type=F32)
            state[...] = jnp.where(number < steps, advanced, state[...])
            return carry

        lax.fori_loop(0, STEPS, step, 0)
        leave, many = OUTGOING[index]
        for slot in range(leave, leave + many):
            arrival(end_land.at[slot], end_sem.at[slot]).wait_recv()
            if slot == 1:
                value = jnp.where(lower, shared[1], state[:, LANES:])
            else:
                value = state[:, 0:LANES]
            result[slot] = value - end_land[slot]
        if not index:
            shared[1] = state[:, LANES:]
        for offset in others:
            leaving(index, *offset).start()
        staying(index).start()

    for index, (comp, count) in enumerate(OUTGOING):
        staying(index).wait()
        for half, dy, dc in others:
            wall_from = halves_in[half] + y_parts[dy] + core_parts[dc]
            arrival(out_ref.at[pl.ds(comp, count), :, pl.ds(pl.multiple_of(wall_from * LANES, LANES), LANES)],
                    out_sem.at[index * WALL + wall_from]).wait_recv()
            leaving(index, half, dy, dc).wait_send()
    for send in sum(sends, end_sends):
        send.wait_send()

    @pl.when(first)
    def _():
        for number in range(len(DETOUR)):
            passing(number)[1].wait_send()

    @pl.when((x == 1) | (x == 2))
    def _():
        arrival(end_land.at[3], end_sem.at[3]).wait_send()


def finish(arrived_ref, start_ref, out_ref):
    lower = lane_tile(ROWS)
    for at in range(0, arrived_ref.shape[2], LANES):
        lanes = slice(at, at + LANES)
        zero, one = packed(arrived_ref[0, :, lanes], arrived_ref[2, :, lanes], lower)
        out_ref[0, :, lanes] = zero + start_ref[0, :, lanes]
        out_ref[1, :, lanes] = one + start_ref[1, :, lanes]
        out_ref[2, :, lanes] = arrived_ref[1, :, lanes] + start_ref[2, :, lanes]


def on_device(start_state, end_state, coupling, inverse_ops, mirror_rows, slab_steps):
    anywhere = pl.BlockSpec(memory_space=pl.ANY)
    start = start_state[0]
    arrived = pl.pallas_call(
        kernel,
        out_shape=jax.ShapeDtypeStruct((3, ROWS, WALL * LANES), F32),
        in_specs=[anywhere] * 5 + [pl.BlockSpec(memory_space=pltpu.SMEM)],
        out_specs=anywhere,
        scratch_shapes=[
            pltpu.VMEM((3, ROWS, WALL * LANES), F32),
            pltpu.VMEM((3, ROWS, WALL * LANES), F32),
            pltpu.VMEM((3, NY + len(DETOUR) * ROWS, LANES), F32),
            pltpu.VMEM((4, NY, LANES), F32),
            pltpu.VMEM((3, NY, LANES), F32),
            pltpu.VMEM((3, NY, LANES), F32),
            pltpu.VMEM((3, NY, LANES), F32),
            pltpu.VMEM((2, NY, NY), F32),
            pltpu.VMEM((NY,), jnp.int32),
            pltpu.VMEM((2, NY, 3 * NY), BF16),
            pltpu.VMEM((3 * NY, 2 * LANES), BF16),
            pltpu.VMEM((NY, NY), BF16),
            pltpu.VMEM((NY, 2 * LANES), F32),
            pltpu.VMEM((2, NY, LANES), F32),
            pltpu.VMEM((3, NY, LANES), F32),
            pltpu.SemaphoreType.DMA((5,)),
            pltpu.SemaphoreType.DMA((len(CHUNKS) + 3,)),
            pltpu.SemaphoreType.DMA((len(CHUNKS) * WALL + len(DETOUR),)),
            pltpu.SemaphoreType.DMA((4,)),
            pltpu.SemaphoreType.DMA((len(CHUNKS) * WALL,)),
            pltpu.SemaphoreType.DMA((len(CHUNKS),)),
            pltpu.SemaphoreType.REGULAR,
        ],
        compiler_params=pltpu.CompilerParams(
            collective_id=0, has_side_effects=True, vmem_limit_bytes=60 * 1024 * 1024
        ),
        name="shooting",
    )(start, end_state[0], coupling[0], inverse_ops, mirror_rows, slab_steps)
    block = pl.BlockSpec((3, ROWS, 8 * LANES), lambda at: (0, 0, at))
    gradient = pl.pallas_call(
        finish,
        out_shape=jax.ShapeDtypeStruct((3, ROWS, WALL * LANES), F32),
        grid=(2,),
        in_specs=[block, block],
        out_specs=block,
        name="finish",
    )(arrived, start)
    return gradient[None]


def solution(mesh):
    in_specs = (
        P("tm", None, "wall", None),
        P("tm", None, None, "wall"),
        P("tm", None, None, "wall"),
        P("wall", None, None),
        P(),
        P("tm"),
    )
    out_specs = P("tm", None, "wall", None)
    return jax.shard_map(
        on_device, mesh=mesh, in_specs=in_specs, out_specs=out_specs, check_vma=False
    )
```

```python
import functools

import jax
import jax.numpy as jnp
from jax import lax
from jax.experimental import pallas as pl
from jax.experimental.pallas import tpu as pltpu
from jax.sharding import PartitionSpec as P

STEPS = 8
NY = 384
ROWS = 24
LANES = 128
WALL = 16
CHUNKS = ((0, 2), (2, 1))
OUTGOING = ((0, 1), (1, 2))
SLOTS = ((0, 1), (2, 1))
SIGN = (1.0, -1.0, 1.0)
DETOUR = ((0, 0), (0, 1), (1, 0))
MESH = pl.DeviceIdType.MESH
F32 = jnp.float32
BF16 = jnp.bfloat16


def place():
    tm = lax.axis_index("tm")
    wall = lax.axis_index("wall")
    x = lax.rem(tm, 4)
    y = lax.rem(lax.div(wall, 2), 4)
    core = lax.rem(wall, 2)
    z = lax.div(wall, 8) * 8 + lax.div(tm, 4)
    return x, y, z, core


def halves(value):
    high = value.astype(BF16)
    return high, (value - high.astype(F32)).astype(BF16)


def permuted(onehot, value):
    high = value.astype(BF16)
    rest = value - high.astype(F32)
    middle, low = halves(rest)
    dot = functools.partial(jnp.dot, preferred_element_type=F32)
    return (dot(onehot, high) + dot(onehot, middle)) + dot(onehot, low)


def lane_tile(rows):
    return lax.broadcasted_iota(jnp.int32, (rows, LANES), 1) < 64


def packed(zero, one, lower):
    return (jnp.where(lower, zero, pltpu.roll(one, 64, 1)),
            jnp.where(lower, pltpu.roll(zero, 64, 1), one))


def kernel(start_ref, end_ref, coupling_ref, ops_ref, mirror_ref, steps_ref, out_ref,
           rows_v, pack, land, end_land, end_send, end_v, coup_v, ops_v, mirror_v, wcat, xcat, onehot, state, shared,
           result, local_sem, send_sem, land_sem, end_sem, out_sem, own_sem, go_sem):
    loads = [
        pltpu.make_async_copy(start_ref, rows_v, local_sem.at[0]),
        pltpu.make_async_copy(mirror_ref, mirror_v, local_sem.at[1]),
        pltpu.make_async_copy(end_ref, end_v, local_sem.at[2]),
        pltpu.make_async_copy(ops_ref, ops_v, local_sem.at[3]),
        pltpu.make_async_copy(coupling_ref, coup_v, local_sem.at[4]),
    ]
    loads[0].start()

    x, y, z, core = place()
    tm, wall = lax.axis_index("tm"), lax.axis_index("wall")
    first = x == 0
    last = x == 3
    tm_before, tm_after = lax.rem(tm + 31, 32), lax.rem(tm + 1, 32)

    def upper(height):
        return lax.div(lax.rem(height, 16), 8) * 8

    def column(x_at, height):
        return lax.rem(height, 8) * 4 + x_at

    y_parts = [lax.rem(y + dy, 4) * 2 for dy in range(4)]
    core_parts = [core, 1 - core]
    here = y_parts[0] + core
    behind = jnp.where(first, 1, 0)
    ahead = jnp.where(last, 1, 0)
    halves_to = {half: upper(z + half + 16 - behind) for half in (8, 0)}
    halves_from = {half: upper(z + half + ahead) for half in (8, 0)}
    halves_in = {half: upper(z + half) for half in (8, 0)}
    next_run = lax.rem(lax.div(tm, 4) + 1, 8) * 4
    run_before = lax.rem(lax.div(tm, 4) + 7, 8) * 4

    turns = x == 1
    leads = turns & (lax.div(tm_before, 4) < 4)
    trails = turns & (lax.div(tm_before, 4) >= 4)
    partner = lax.rem(tm + 16, 32)

    barrier = pltpu.get_barrier_semaphore()

    def greet(*device):
        pl.semaphore_signal(barrier, inc=1, device_id=device, device_id_type=MESH)

    for other in range(WALL):
        greet(tm_after, other)
    greet(tm_before, wall)

    @pl.when(trails)
    def _():
        greet(partner, wall)

    @pl.when(first)
    def _():
        for dy, dc in DETOUR:
            greet(column(0, z + 2), upper(z + 2) + y_parts[-dy] + core_parts[dc])
        greet(run_before + 1, wall)
        greet(run_before + 2, wall)

    @pl.when(last)
    def _():
        greet(column(0, z + 7), upper(z + 7) + here)

    @pl.when(x == 1)
    def _():
        greet(tm + 2, wall)

    for load in loads[1:]:
        load.start()
    loads[0].wait()
    narrow = lane_tile(ROWS)

    def pack_columns(number, carry):
        lanes = pl.ds(pl.multiple_of(number * LANES, LANES), LANES)
        pack[0, :, lanes], pack[2, :, lanes] = packed(rows_v[0, :, lanes], rows_v[1, :, lanes], narrow)
        pack[1, :, lanes] = rows_v[2, :, lanes]
        return carry

    lax.fori_loop(0, WALL, pack_columns, 0, unroll=4)
    pl.semaphore_wait(barrier, jnp.where(first, WALL + 5, WALL + 2) + jnp.where(leads, 1, 0))

    def first_hop(index, half, dy, dc):
        wall_to = halves_to[half] + y_parts[dy] + core_parts[dc]
        lanes = pl.multiple_of(wall_to * LANES, LANES)
        tm_to, row, sem = tm_before, wall * ROWS, index * WALL + wall
        comp, count = CHUNKS[index]
        if half and (dy, dc) in DETOUR:
            comp, count = 0, 3
            number = DETOUR.index((dy, dc))
            tm_to = jnp.where(first, column(0, z + 14), tm_to)
            wall_to = jnp.where(first, upper(z + 14) + y_parts[dy] + core_parts[dc], wall_to)
            row = jnp.where(first, NY + number * ROWS, row)
            sem = jnp.where(first, len(CHUNKS) * WALL + number, sem)
        return pltpu.make_async_remote_copy(
            pack.at[pl.ds(comp, count), :, pl.ds(lanes, LANES)],
            land.at[pl.ds(comp, count), pl.ds(pl.multiple_of(row, 8), ROWS), :],
            send_sem.at[index], land_sem.at[sem], device_id=(tm_to, wall_to), device_id_type=MESH)

    pairs = [(dy, dc) for dy in range(4) for dc in range(2)]
    plain = [(half, dy, dc) for half in (8, 0) for dy, dc in pairs if not half or (dy, dc) not in DETOUR]
    sends = [[first_hop(0, 8, dy, dc) for dy, dc in DETOUR] + [first_hop(0, *offset) for offset in plain]]
    sends += [[first_hop(index, *offset) for offset in plain] for index in range(1, len(CHUNKS))]
    @pl.when(trails)
    def _():
        pl.semaphore_wait(go_sem, 1)

    for send in sends[0]:
        send.start()

    @pl.when(leads)
    def _():
        pl.semaphore_signal(go_sem, inc=1, device_id=(partner, wall), device_id_type=MESH)

    lower = lane_tile(NY)
    signs = [jnp.where(lower, SIGN[0], SIGN[1]), SIGN[2], jnp.where(lower, SIGN[0], SIGN[1])]
    source = lax.broadcasted_iota(jnp.int32, (NY, NY), 0)
    loads[1].wait()
    onehot[...] = jnp.where(source == mirror_v[...].reshape(1, NY), 1.0, 0.0).astype(BF16)
    loads[2].wait()
    kept = end_v[2]
    end_v[0], end_v[2] = packed(end_v[0], end_v[1], lower)
    end_v[1] = kept
    end_sends = []
    for comp in (1, 2, 0):
        end_send[comp] = permuted(onehot[...], end_v[comp]) * signs[comp]
        slot, tm_to = comp, tm_after
        if comp:
            tm_to = jnp.where(last, tm - (3 - comp), tm_to)
            slot = jnp.where(last, 3, comp)
        send = pltpu.make_async_remote_copy(
            end_send.at[comp], end_land.at[slot], send_sem.at[len(CHUNKS)], end_sem.at[slot],
            device_id=(tm_to, wall), device_id_type=MESH)
        send.start()
        end_sends.append(send)

    def arrival(ref, sem):
        return pltpu.make_async_remote_copy(
            ref, ref, send_sem.at[len(CHUNKS) + 1], sem, device_id=(tm, wall), device_id_type=MESH)

    def passing(number):
        dy, dc = DETOUR[number]
        wall_from = upper(z + 2) + y_parts[-dy] + core_parts[dc]
        held = land.at[:, pl.ds(NY + number * ROWS, ROWS), :]
        return held, pltpu.make_async_remote_copy(
            held, land.at[:, pl.ds(pl.multiple_of(wall_from * ROWS, 8), ROWS), :],
            send_sem.at[len(CHUNKS) + 1], land_sem.at[wall_from],
            device_id=(column(3, z + 9), upper(z + 9) + here), device_id_type=MESH)

    @pl.when(first)
    def _():
        for number in range(len(DETOUR)):
            held, copy = passing(number)
            arrival(held, land_sem.at[len(CHUNKS) * WALL + number]).wait_recv()
            copy.start()

    loads[3].wait()
    for group in range(2):
        high, low = halves(ops_v[group])
        wcat[group, :, 0:NY] = high
        wcat[group, :, NY:2 * NY] = low
        wcat[group, :, 2 * NY:3 * NY] = high
    loads[4].wait()
    kept = coup_v[2]
    coup_v[0], coup_v[2] = packed(coup_v[0], coup_v[1], lower)
    coup_v[1] = kept

    for send in sends[1]:
        send.start()

    @pl.when((x == 1) | (x == 2))
    def _():
        arrival(end_land.at[3], end_sem.at[3]).wait_recv()
        pltpu.make_async_remote_copy(
            end_land.at[3], end_land.at[x], send_sem.at[len(CHUNKS) + 1], end_sem.at[x],
            device_id=(next_run, wall), device_id_type=MESH).start()


    def leaving(index, half, dy, dc):
        comp, count = OUTGOING[index]
        wall_to = halves_in[half] + y_parts[dy] + core_parts[dc]
        return pltpu.make_async_remote_copy(
            result.at[pl.ds(comp, count), pl.ds(pl.multiple_of(wall_to * ROWS, 8), ROWS), :],
            out_ref.at[pl.ds(comp, count), :, pl.ds(pl.multiple_of(wall * LANES, LANES), LANES)],
            send_sem.at[len(CHUNKS) + 2], out_sem.at[index * WALL + wall], device_id=(tm, wall_to), device_id_type=MESH)

    def staying(index):
        comp, count = OUTGOING[index]
        return pltpu.make_async_copy(
            result.at[pl.ds(comp, count), pl.ds(pl.multiple_of(wall * ROWS, 8), ROWS), :],
            out_ref.at[pl.ds(comp, count), :, pl.ds(pl.multiple_of(wall * LANES, LANES), LANES)],
            own_sem.at[index])

    steps = steps_ref[0]
    others = [(half, dy, dc) for half in (8, 0) for dy, dc in pairs if half or dy or dc]
    for index, (comp, count) in enumerate(CHUNKS):
        def landed(half, dy, dc, comp, count):
            wall_from = halves_from[half] + y_parts[-dy] + core_parts[dc]
            arrival(land.at[pl.ds(comp, count), pl.ds(pl.multiple_of(wall_from * ROWS, 8), ROWS), :],
                    land_sem.at[index * WALL + wall_from]).wait_recv()

        if index == 0:
            for dy, dc in DETOUR:
                landed(8, dy, dc, 0, 3)
        for offset in plain:
            landed(*offset, comp, count)
        if 1 < index + 2 < len(CHUNKS):
            for send in sends[index + 2]:
                send.start()
        fresh = SLOTS[index] if not index else SLOTS[index][:1]
        for at, slot in enumerate(SLOTS[index]):
            lanes = slice(at * LANES, (at + 1) * LANES)
            if slot in fresh:
                state[:, lanes] = end_v[slot] - permuted(onehot[...], land[slot, 0:NY, :]) * signs[slot]
                if slot == 1:
                    shared[0] = state[:, lanes]
            else:
                state[:, lanes] = shared[0]

        def step(number, carry, index=index):
            for at, slot in enumerate(SLOTS[index]):
                lanes = slice(at * LANES, (at + 1) * LANES)
                high, low = halves(coup_v[slot] * state[:, lanes])
                xcat[0:NY, lanes] = high
                xcat[NY:2 * NY, lanes] = high
                xcat[2 * NY:3 * NY, lanes] = low
            advanced = jnp.dot(wcat[index], xcat[...], preferred_element_type=F32)
            state[...] = jnp.where(number < steps, advanced, state[...])
            return carry

        lax.fori_loop(0, STEPS, step, 0)
        leave, many = OUTGOING[index]
        for slot in range(leave, leave + many):
            arrival(end_land.at[slot], end_sem.at[slot]).wait_recv()
            if slot == 1:
                value = jnp.where(lower, shared[1], state[:, LANES:])
            else:
                value = state[:, 0:LANES]
            result[slot] = value - end_land[slot]
        if not index:
            shared[1] = state[:, LANES:]
        for offset in others:
            leaving(index, *offset).start()
        staying(index).start()

    for index, (comp, count) in enumerate(OUTGOING):
        staying(index).wait()
        for half, dy, dc in others:
            wall_from = halves_in[half] + y_parts[dy] + core_parts[dc]
            arrival(out_ref.at[pl.ds(comp, count), :, pl.ds(pl.multiple_of(wall_from * LANES, LANES), LANES)],
                    out_sem.at[index * WALL + wall_from]).wait_recv()
            leaving(index, half, dy, dc).wait_send()
    for send in sum(sends, end_sends):
        send.wait_send()

    @pl.when(first)
    def _():
        for number in range(len(DETOUR)):
            passing(number)[1].wait_send()

    @pl.when((x == 1) | (x == 2))
    def _():
        arrival(end_land.at[3], end_sem.at[3]).wait_send()


def finish(arrived_ref, start_ref, out_ref):
    lower = lane_tile(ROWS)
    for at in range(0, arrived_ref.shape[2], LANES):
        lanes = slice(at, at + LANES)
        zero, one = packed(arrived_ref[0, :, lanes], arrived_ref[2, :, lanes], lower)
        out_ref[0, :, lanes] = zero + start_ref[0, :, lanes]
        out_ref[1, :, lanes] = one + start_ref[1, :, lanes]
        out_ref[2, :, lanes] = arrived_ref[1, :, lanes] + start_ref[2, :, lanes]


def on_device(start_state, end_state, coupling, inverse_ops, mirror_rows, slab_steps):
    anywhere = pl.BlockSpec(memory_space=pl.ANY)
    start = start_state[0]
    arrived = pl.pallas_call(
        kernel,
        out_shape=jax.ShapeDtypeStruct((3, ROWS, WALL * LANES), F32),
        in_specs=[anywhere] * 5 + [pl.BlockSpec(memory_space=pltpu.SMEM)],
        out_specs=anywhere,
        scratch_shapes=[
            pltpu.VMEM((3, ROWS, WALL * LANES), F32),
            pltpu.VMEM((3, ROWS, WALL * LANES), F32),
            pltpu.VMEM((3, NY + len(DETOUR) * ROWS, LANES), F32),
            pltpu.VMEM((4, NY, LANES), F32),
            pltpu.VMEM((3, NY, LANES), F32),
            pltpu.VMEM((3, NY, LANES), F32),
            pltpu.VMEM((3, NY, LANES), F32),
            pltpu.VMEM((2, NY, NY), F32),
            pltpu.VMEM((NY,), jnp.int32),
            pltpu.VMEM((2, NY, 3 * NY), BF16),
            pltpu.VMEM((3 * NY, 2 * LANES), BF16),
            pltpu.VMEM((NY, NY), BF16),
            pltpu.VMEM((NY, 2 * LANES), F32),
            pltpu.VMEM((2, NY, LANES), F32),
            pltpu.VMEM((3, NY, LANES), F32),
            pltpu.SemaphoreType.DMA((5,)),
            pltpu.SemaphoreType.DMA((len(CHUNKS) + 3,)),
            pltpu.SemaphoreType.DMA((len(CHUNKS) * WALL + len(DETOUR),)),
            pltpu.SemaphoreType.DMA((4,)),
            pltpu.SemaphoreType.DMA((len(CHUNKS) * WALL,)),
            pltpu.SemaphoreType.DMA((len(CHUNKS),)),
            pltpu.SemaphoreType.REGULAR,
        ],
        compiler_params=pltpu.CompilerParams(
            collective_id=0, has_side_effects=True, vmem_limit_bytes=60 * 1024 * 1024
        ),
        name="shooting",
    )(start, end_state[0], coupling[0], inverse_ops, mirror_rows, slab_steps)
    block = pl.BlockSpec((3, ROWS, 8 * LANES), lambda at: (0, 0, at))
    gradient = pl.pallas_call(
        finish,
        out_shape=jax.ShapeDtypeStruct((3, ROWS, WALL * LANES), F32),
        grid=(2,),
        in_specs=[block, block],
        out_specs=block,
        name="finish",
    )(arrived, start)
    return gradient[None]


def solution(mesh):
    in_specs = (
        P("tm", None, "wall", None),
        P("tm", None, None, "wall"),
        P("tm", None, None, "wall"),
        P("wall", None, None),
        P(),
        P("tm"),
    )
    out_specs = P("tm", None, "wall", None)
    return jax.shard_map(
        on_device, mesh=mesh, in_specs=in_specs, out_specs=out_specs, check_vma=False
    )
```
